256 devices in a mesh: seq: 32 (over y, z), head: 8 (over x, core).
Axes of the slice: x: 4, y: 4, z: 8, core: 2. Of those that a mesh axis runs over, the one named last changes fastest.
Arguments:
- queries: bfloat16 [65536, 4096], P('seq', 'head'), may hold values from -5 to 5
- keys: bfloat16 [65536, 1024], P('seq', 'head'), may hold values from -5 to 5
- values: bfloat16 [65536, 1024], P('seq', 'head'), may hold values from -6 to 6
- grad_out: bfloat16 [65536, 4096], P('seq', 'head'), may hold values from -6 to 6
- vertical: int32 [32], replicated, may hold values from 0 to 15
- columns: int32 [512, 2], P('seq'), may hold values from 0 to 31, as said below
- offsets: int32 [512, 2], P('seq'), may hold values from 1 to 32
Outputs:
- grad_queries: bfloat16 [65536, 4096], P(('seq', 'head'))
- grad_keys: bfloat16 [65536, 1024], P(('seq', 'head'))
- grad_values: bfloat16 [65536, 1024], P(('seq', 'head'))
The draws below stay inside these ranges and needn't reach their ends.
Inputs may be any that keep to these rules, and one draw needn't show every extreme that they name: `columns`: entry c names vertical column c, held by seq index c; an entry of query block i is below (i // 16 + 1).
All inputs are finite; a program needn't handle non-finite values.
Results may differ from the reference program's by a relative error of at most 0.014.
Values may be sent and summed in bfloat16 or wider, within the bound.
A program may use at most 128 MiB of HBM per device.

```python
import math
import jax
import jax.numpy as jnp
from jax import lax

H = 32
KVH = 8
HD = 128
BLK = 128
VERT_DEV = 1
TOK_DEV = 2048
TOKENS = 65536
NB = 512
NV = 32


def base_field(key, width):
    return jnp.clip(jax.random.normal(key, (TOKENS, width), jnp.float32), -5.0, 5.0)


def draw_queries(key, part):
    field = base_field(jax.random.fold_in(key, 11), H * HD)
    return field.astype(jnp.bfloat16)


def draw_keys(key, part):
    field = base_field(jax.random.fold_in(key, 12), KVH * HD)
    return field.astype(jnp.bfloat16)


def draw_columns(key, part):
    rows = jnp.arange(NB)
    upper = (rows // (TOK_DEV // BLK) + 1) * VERT_DEV
    return jax.random.randint(key, (NB, 2), 0, upper[:, None]).astype(jnp.int32)


def place_ends(entries, key, smallest, largest):
    extent = entries.shape
    spot = [jax.random.randint(jax.random.fold_in(key, axis), (), 0, extent[axis]) for axis in range(len(extent))]
    entries = entries.at[tuple(spot)].set(smallest)
    longest = extent.index(max(extent))
    spot[longest] = (spot[longest] + 1) % extent[longest]
    return entries.at[tuple(spot)].set(largest)


def steps_of(key, shape, pieces, low, largest):
    level = 1.0
    for axis_at, parts in pieces:
        steps = jax.random.uniform(jax.random.fold_in(jax.random.fold_in(key, 6), axis_at), (parts,), jnp.float32, low / len(pieces), largest / len(pieces))
        level = level * jnp.repeat(jnp.exp(steps), shape[axis_at] // parts).reshape((-1,) + (1,) * (len(shape) - 1 - axis_at))
    return level


def centred(own_key, shape, spread, reach, pieces=(), kind=jnp.bfloat16):
    drawn = jax.random.normal(own_key, shape, jnp.float32) * spread
    if len(pieces) > 0:
        drawn = steps_of(own_key, shape, pieces, -0.22, 0.18) * drawn
    return jnp.clip(drawn, min=-reach, max=reach).astype(kind)


def setup_inputs(seed: int = 0) -> dict:
    streams_of = jax.random.split(jax.random.key(seed), 8)
    queries = draw_queries(jax.random.fold_in(streams_of[7], 71), 0)
    keys = draw_keys(jax.random.fold_in(streams_of[7], 71), 0)
    values = centred(streams_of[2], (TOKENS, KVH * HD), 1.0, 6.0, ((0, 32), (1, 8)))
    grad_out = centred(streams_of[3], (TOKENS, H * HD), 1.0, 6.0, ((0, 32), (1, 8)))
    vertical = place_ends(jax.random.randint(streams_of[4], (NV,), 0, TOK_DEV // BLK), jax.random.fold_in(streams_of[4], 1), 0, (TOK_DEV // BLK) - 1).astype(jnp.int32)
    columns = draw_columns(jax.random.fold_in(streams_of[7], 71), 0)
    offsets = place_ends(jax.random.randint(streams_of[6], (NB, 2), 1, 2 * (TOK_DEV // BLK) + 1), jax.random.fold_in(streams_of[6], 1), 1, (2 * (TOK_DEV // BLK) + 1) - 1).astype(jnp.int32)
    return {"queries": queries, "keys": keys, "values": values, "grad_out": grad_out, "vertical": vertical, "columns": columns, "offsets": offsets}


def reference(queries, keys, values, grad_out, vertical, columns, offsets):
    tokens = queries.shape[0]
    block_count = tokens // BLK
    local_blocks = TOK_DEV // BLK
    group_size = H // KVH
    score_scale = 1.0 / math.sqrt(HD)
    query_blocks = queries.reshape(block_count, BLK, KVH, group_size, HD)
    grad_blocks = grad_out.reshape(block_count, BLK, KVH, group_size, HD)
    key_blocks = keys.reshape(block_count, BLK, KVH, HD)
    value_blocks = values.reshape(block_count, BLK, KVH, HD)
    vert_ids = jnp.arange(vertical.shape[0], dtype=jnp.int32)
    vert_global = (vert_ids // VERT_DEV * local_blocks + vertical).astype(jnp.int32)
    positions = jnp.arange(BLK)
    causal = positions[None, :] <= positions[:, None]

    def block_step(accums, block_index):
        acc_keys, acc_values = accums
        block_index = block_index.astype(jnp.int32)
        slot_blocks = jnp.stack([jnp.zeros((), jnp.int32), block_index, block_index - offsets[block_index, 0], block_index - offsets[block_index, 1], vert_global[columns[block_index, 0]], vert_global[columns[block_index, 1]]]).astype(jnp.int32)
        slot_flags = []
        for slot_number in range(6):
            current = slot_blocks[slot_number]
            slot_good = (current >= 0) & (current <= block_index)
            for prior in range(slot_number):
                slot_good = slot_good & (current != slot_blocks[prior])
            slot_flags.append(slot_good)
        slot_valid = jnp.stack(slot_flags)
        safe_blocks = jnp.clip(slot_blocks, 0, block_count - 1).astype(jnp.int32)
        key_rows = key_blocks[safe_blocks].astype(jnp.float32)
        value_rows = value_blocks[safe_blocks].astype(jnp.float32)
        query_rows = query_blocks[block_index].astype(jnp.float32)
        grad_rows = grad_blocks[block_index].astype(jnp.float32)
        scores = jnp.einsum('qkgd,sckd->kgqsc', query_rows, key_rows) * score_scale
        earlier = slot_blocks < block_index
        visible = slot_valid[None, :, None] & (earlier[None, :, None] | causal[:, None, :])
        visible = visible[None, None]
        masked = jnp.where(visible, scores, -1e+30)
        row_top = lax.optimization_barrier(jnp.max(masked, axis=(3, 4), keepdims=True))
        row_total = lax.optimization_barrier(jnp.sum(jnp.where(visible, jnp.exp(masked - row_top), 0.0), axis=(3, 4), keepdims=True))
        prob_full = jnp.where(visible, jnp.exp(masked - (row_top + jnp.log(row_total))), 0.0)
        grad_prob = jnp.einsum('qkgd,sckd->kgqsc', grad_rows, value_rows)
        row_delta = lax.optimization_barrier(jnp.sum(prob_full * grad_prob, axis=(3, 4), keepdims=True))
        dscore = (prob_full * (grad_prob - row_delta) * score_scale).astype(jnp.bfloat16)
        prob_half = prob_full.astype(jnp.bfloat16)
        grad_query = jnp.einsum('kgqsc,sckd->qkgd', dscore.astype(jnp.float32), key_rows).astype(jnp.bfloat16)
        key_terms = jnp.einsum('kgqsc,qkgd->sckd', dscore.astype(jnp.float32), query_rows)
        value_terms = jnp.einsum('kgqsc,qkgd->sckd', prob_half.astype(jnp.float32), grad_rows)
        acc_keys = acc_keys.at[safe_blocks].add(key_terms)
        acc_values = acc_values.at[safe_blocks].add(value_terms)
        return ((acc_keys, acc_values), grad_query)
    zero_acc = jnp.zeros((block_count, BLK, KVH, HD), jnp.float32)
    (acc_keys, acc_values), grad_query = lax.scan(block_step, (zero_acc, zero_acc), jnp.arange(block_count, dtype=jnp.int32))
    grad_queries = grad_query.reshape(tokens, H * HD)
    grad_keys = acc_keys.reshape(tokens, KVH * HD).astype(jnp.bfloat16)
    grad_values = acc_values.reshape(tokens, KVH * HD).astype(jnp.bfloat16)
    return (grad_queries, grad_keys, grad_values)
```

```python
import functools
import math

import jax
import jax.numpy as jnp
from jax import lax
from jax.experimental import pallas as pl
from jax.experimental.pallas import tpu as pltpu
from jax.sharding import PartitionSpec as P

HD = 128
BLK = 128
ZDIM = 8
CHUNKS = 4
NEG = -1e30
BIG = 1e30
MESH = pl.DeviceIdType.MESH
ANY = pl.ANY


def peers_of(ydim, zdim):
    s = lax.axis_index("seq")
    total = ydim * zdim
    y, z = s // zdim, lax.rem(s, zdim)
    nxt = lax.rem(s + 1, total)
    prv = lax.rem(s + total - 1, total)
    zl = y * zdim + lax.rem(z + zdim - 1, zdim)
    zr = y * zdim + lax.rem(z + 1, zdim)
    yu = lax.rem(y + 1, ydim) * zdim + z
    yd = lax.rem(y + ydim - 1, ydim) * zdim + z
    return s, y, z, nxt, prv, zl, zr, yu, yd


def send(src, dst, send_sem, recv_sem, seq, head):
    copy = pltpu.make_async_remote_copy(
        src_ref=src,
        dst_ref=dst,
        send_sem=send_sem,
        recv_sem=recv_sem,
        device_id={"seq": seq, "head": head},
        device_id_type=MESH,
    )
    copy.start()
    return copy


def landed(ref, send_sem, recv_sem, seq, head):
    pltpu.make_async_remote_copy(
        src_ref=ref,
        dst_ref=ref,
        send_sem=send_sem,
        recv_sem=recv_sem,
        device_id={"seq": seq, "head": head},
        device_id_type=MESH,
    ).wait_recv()


def sent(src, dst, send_sem, recv_sem, seq, head):
    pltpu.make_async_remote_copy(
        src_ref=src,
        dst_ref=dst,
        send_sem=send_sem,
        recv_sem=recv_sem,
        device_id={"seq": seq, "head": head},
        device_id_type=MESH,
    ).wait_send()


def meet(pairs):
    barrier = pltpu.get_barrier_semaphore()
    for seq, head in pairs:
        pl.semaphore_signal(
            barrier, inc=1, device_id={"seq": seq, "head": head}, device_id_type=MESH
        )
    pl.semaphore_wait(barrier, len(pairs))


def gather_kernel(
    ydim, zdim, k, v, item, pk, pv, bk, bv, far,
    local_sem, own_s, own_r, rel_s, rel_r, z_s, z_r, y_s, y_r, w_s, w_r, sink_s, sink_r,
):
    s, y, z, nxt, prv, zl, zr, yu, yd = peers_of(ydim, zdim)
    h = lax.axis_index("head")
    total = ydim * zdim
    step = k.shape[0] // CHUNKS
    sink = far.at[total]
    meet([(nxt, h), (prv, h), (zl, h), (zr, h), (yu, h), (yd, h)])

    own = []
    for c in range(CHUNKS):
        part = pl.ds(c * step, step)
        own.append(send(k.at[part], pk.at[part], own_s.at[0, c], own_r.at[0, c], nxt, h))
        own.append(send(v.at[part], pv.at[part], own_s.at[1, c], own_r.at[1, c], nxt, h))
    keep = pltpu.make_async_copy(item, far.at[s], local_sem.at[0])
    keep.start()
    sink_k = pltpu.make_async_copy(k.at[0], far.at[total, 0], local_sem.at[1])
    sink_v = pltpu.make_async_copy(v.at[0], far.at[total, 1], local_sem.at[2])

    @pl.when(s == 0)
    def _():
        sink_k.start()
        sink_v.start()
        sink_k.wait()
        sink_v.wait()

    def item_at(row, t):
        return lax.rem(row + ydim, ydim) * zdim + lax.rem(z + t, zdim)

    def sink_send(origin, slot, seq):
        @pl.when(origin == 0)
        def _():
            send(sink, sink, sink_s.at[slot], sink_r, seq, h)

    def sink_wait(origin):
        @pl.when(origin == 0)
        def _():
            landed(sink, sink_s.at[0], sink_r, prv, h)

    def sink_sent(origin, slot):
        @pl.when(origin == 0)
        def _():
            sent(sink, sink, sink_s.at[slot], sink_r, prv, h)

    flying = []
    for t in range(zdim):
        origin = item_at(y, t)
        src = item if t == 0 else far.at[origin]
        if t > 0:
            landed(far.at[origin], z_s.at[t - 1], z_r.at[t - 1], zr, h)
            sink_wait(origin)
        if t < zdim - 1:
            flying.append(send(src, far.at[origin], z_s.at[t], z_r.at[t], zl, h))
            sink_send(origin, 0, zl)
        flying.append(send(src, far.at[origin], y_s.at[0, t], y_r.at[0, t], yu, h))
        sink_send(origin, 1, yu)
        flying.append(send(src, far.at[origin], y_s.at[1, t], y_r.at[1, t], yd, h))
        sink_send(origin, 2, yd)

    for c in range(CHUNKS):
        part = pl.ds(c * step, step)
        landed(pk.at[part], own_s.at[0, c], own_r.at[0, c], prv, h)
        flying.append(send(pk.at[part], bk.at[part], rel_s.at[0, c], rel_r.at[0, c], nxt, h))
        landed(pv.at[part], own_s.at[1, c], own_r.at[1, c], prv, h)
        flying.append(send(pv.at[part], bv.at[part], rel_s.at[1, c], rel_r.at[1, c], nxt, h))

    for t in range(zdim):
        below = item_at(y - 1, t)
        above = item_at(y + 1, t)
        landed(far.at[below], y_s.at[0, t], y_r.at[0, t], yd, h)
        sink_wait(below)
        landed(far.at[above], y_s.at[1, t], y_r.at[1, t], yu, h)
        sink_wait(above)
        origin, seq = (below, yu) if t % 2 == 0 else (above, yd)
        flying.append(send(far.at[origin], far.at[origin], w_s.at[t], w_r.at[t], seq, h))
        sink_send(origin, 3, seq)

    for t in range(zdim):
        origin = item_at(y + 2, t)
        landed(far.at[origin], w_s.at[t], w_r.at[t], yd, h)
        sink_wait(origin)
    for c in range(CHUNKS):
        part = pl.ds(c * step, step)
        landed(bk.at[part], rel_s.at[0, c], rel_r.at[0, c], prv, h)
        landed(bv.at[part], rel_s.at[1, c], rel_r.at[1, c], prv, h)
    for copy in own + flying:
        copy.wait_send()
    for t in range(zdim):
        origin = item_at(y, t)
        if t < zdim - 1:
            sink_sent(origin, 0)
        sink_sent(origin, 1)
        sink_sent(origin, 2)
        sink_sent(item_at(y - 1, t) if t % 2 == 0 else item_at(y + 1, t), 3)
    keep.wait()


def gather(ydim, zdim, k, v, item):
    blocks = jax.ShapeDtypeStruct(k.shape, k.dtype)
    total = ydim * zdim
    dma = pltpu.SemaphoreType.DMA
    return pl.pallas_call(
        functools.partial(gather_kernel, ydim, zdim),
        out_shape=(
            blocks, blocks, blocks, blocks,
            jax.ShapeDtypeStruct((total + 1,) + item.shape, item.dtype),
        ),
        in_specs=[pl.BlockSpec(memory_space=ANY)] * 2 + [pl.BlockSpec(memory_space=pltpu.VMEM)],
        out_specs=[pl.BlockSpec(memory_space=ANY)] * 5,
        scratch_shapes=[
            dma((3,)),
            dma((2, CHUNKS)), dma((2, CHUNKS)), dma((2, CHUNKS)), dma((2, CHUNKS)),
            dma((zdim,)), dma((zdim,)),
            dma((2, zdim)), dma((2, zdim)),
            dma((zdim,)), dma((zdim,)),
            dma((4,)), dma,
        ],
        compiler_params=pltpu.CompilerParams(collective_id=0, has_side_effects=True),
        name="gather_blocks",
    )(k, v, item)


def attend_kernel(
    vert, cols, offs, pos,
    q_ref, g_ref, bk, bv, pk, pv, ok, ov, far,
    dq_ref, gbk, gbv, gpk, gpv, gok, gov, gfar,
    kpool, vpool, acck, accv, s_buf, p_buf, e_buf, d_buf, h_buf, sems,
):
    b = pl.program_id(0)
    nb = pl.num_programs(0)
    local = ok.shape[0]
    nfar = far.shape[0]
    group = q_ref.shape[1] // HD
    near = 3 * local
    rows = group * BLK

    @pl.when(b == 0)
    def _():
        copies = []
        for n, (ksrc, vsrc) in enumerate(((bk, bv), (pk, pv), (ok, ov))):
            part = pl.ds(n * local, local)
            copies.append(pltpu.make_async_copy(ksrc, kpool.at[part], sems.at[2 * n]))
            copies.append(pltpu.make_async_copy(vsrc, vpool.at[part], sems.at[2 * n + 1]))
        part = pl.ds(near, nfar)
        copies.append(pltpu.make_async_copy(far.at[:, 0], kpool.at[part], sems.at[6]))
        copies.append(pltpu.make_async_copy(far.at[:, 1], vpool.at[part], sems.at[7]))
        for copy in copies:
            copy.start()
        acck[...] = jnp.zeros_like(acck)
        accv[...] = jnp.zeros_like(accv)
        for copy in copies:
            copy.wait()

    me = pos[0] * local + b
    o0, o1 = offs[2 * b], offs[2 * b + 1]
    c0, c1 = cols[2 * b], cols[2 * b + 1]
    b2, b3 = me - o0, me - o1
    b4, b5 = c0 * local + vert[c0], c1 * local + vert[c1]
    index = [
        near + nfar - 1,
        2 * local + b,
        2 * local + b - o0,
        2 * local + b - o1,
        near + c0,
        near + c1,
    ]
    live = [
        me > 0,
        None,
        (b2 > 0) & (b2 < me),
        (b3 > 0) & (b3 < me) & (b3 != b2),
        (b4 > 0) & (b4 < me) & (b4 != b2) & (b4 != b3),
        (b5 > 0) & (b5 < me) & (b5 != b2) & (b5 != b3) & (b5 != b4),
    ]
    scale = 1.0 / math.sqrt(HD)
    rate = scale * math.log2(math.e)
    nt = (((1,), (1,)), ((), ()))
    f32 = jnp.float32

    qs = jnp.concatenate([q_ref[:, g * HD : (g + 1) * HD] for g in range(group)], axis=0)
    gs = jnp.concatenate([g_ref[:, g * HD : (g + 1) * HD] for g in range(group)], axis=0)
    key_at = lax.broadcasted_iota(jnp.int32, (BLK, rows), 0)
    row_at = lax.broadcasted_iota(jnp.int32, (BLK, rows), 1) & (BLK - 1)
    causal = key_at <= row_at

    top = jnp.full((1, rows), NEG, f32)
    for j in range(6):
        part = pl.ds(j * BLK, BLK)
        kj = kpool[index[j]]
        h_buf[part, :] = kj
        sj = lax.dot_general(kj, qs, nt, preferred_element_type=f32)
        if j == 1:
            sj = jnp.where(causal, sj, NEG)
        s_buf[part, :] = sj
        best = jnp.max(sj, axis=0, keepdims=True)
        if live[j] is not None:
            best = jnp.where(live[j], best, NEG)
        top = jnp.maximum(top, best)
        d_buf[part, :] = lax.dot_general(vpool[index[j]], gs, nt, preferred_element_type=f32)
    total = jnp.zeros((1, rows), f32)
    cross = jnp.zeros((1, rows), f32)
    for j in range(6):
        part = pl.ds(j * BLK, BLK)
        base = top if live[j] is None else jnp.where(live[j], top, BIG)
        ej = jnp.exp2((s_buf[part, :] - base) * rate)
        s_buf[part, :] = ej
        total = total + jnp.sum(ej, axis=0, keepdims=True)
        cross = cross + jnp.sum(ej * d_buf[part, :], axis=0, keepdims=True)
    inv = 1.0 / total
    delta = cross * inv
    inv_scaled = inv * scale
    for j in range(6):
        part = pl.ds(j * BLK, BLK)
        ej = s_buf[part, :]
        p_buf[part, :] = (ej * inv).astype(jnp.bfloat16)
        e_buf[part, :] = ((ej * inv_scaled) * (d_buf[part, :] - delta)).astype(jnp.bfloat16)
    for j in range(6):
        part = pl.ds(j * BLK, BLK)
        acck[index[j]] += jnp.dot(e_buf[part, :], qs, preferred_element_type=f32)
        accv[index[j]] += jnp.dot(p_buf[part, :], gs, preferred_element_type=f32)
    dq = lax.dot_general(
        h_buf[...], e_buf[...], (((0,), (0,)), ((), ())), preferred_element_type=f32
    )
    for g in range(group):
        dq_ref[:, g * HD : (g + 1) * HD] = (
            dq[:, g * BLK : (g + 1) * BLK].T.astype(jnp.bfloat16)
        )

    @pl.when(b == nb - 1)
    def _():
        half = jnp.bfloat16
        gbk[...] = acck[0:local].astype(half)
        gbv[...] = accv[0:local].astype(half)
        gpk[...] = acck[local : 2 * local]
        gpv[...] = accv[local : 2 * local]
        gok[...] = acck[2 * local : near]
        gov[...] = accv[2 * local : near]
        gfar[:, 0] = acck[near : near + nfar].astype(half)
        gfar[:, 1] = accv[near : near + nfar].astype(half)


def attend(vertical, columns, offsets, pos, q, g, bk, bv, pk, pv, k, v, far):
    local = k.shape[0]
    nfar = far.shape[0]
    pool = 3 * local + nfar
    width = q.shape[1]
    rows = width // HD * BLK
    row_spec = pl.BlockSpec((BLK, width), lambda b, *_: (b, 0))
    hbm = pl.BlockSpec(memory_space=ANY)
    f32, half = jnp.float32, jnp.bfloat16

    def whole(shape):
        return pl.BlockSpec(shape, lambda b, *_: (0,) * len(shape), pipeline_mode=pl.Buffered(1))

    near_shape = (local, BLK, HD)
    far_shape = (nfar, 2, BLK, HD)
    return pl.pallas_call(
        attend_kernel,
        out_shape=(
            jax.ShapeDtypeStruct(q.shape, half),
            jax.ShapeDtypeStruct(near_shape, half),
            jax.ShapeDtypeStruct(near_shape, half),
            jax.ShapeDtypeStruct(near_shape, f32),
            jax.ShapeDtypeStruct(near_shape, f32),
            jax.ShapeDtypeStruct(near_shape, f32),
            jax.ShapeDtypeStruct(near_shape, f32),
            jax.ShapeDtypeStruct(far_shape, half),
        ),
        grid_spec=pltpu.PrefetchScalarGridSpec(
            num_scalar_prefetch=4,
            grid=(local,),
            in_specs=[row_spec, row_spec] + [hbm] * 7,
            out_specs=[row_spec] + [whole(near_shape)] * 6 + [whole(far_shape)],
            scratch_shapes=[
                pltpu.VMEM((pool, BLK, HD), half),
                pltpu.VMEM((pool, BLK, HD), half),
                pltpu.VMEM((pool, BLK, HD), f32),
                pltpu.VMEM((pool, BLK, HD), f32),
                pltpu.VMEM((6 * BLK, rows), f32),
                pltpu.VMEM((6 * BLK, rows), half),
                pltpu.VMEM((6 * BLK, rows), half),
                pltpu.VMEM((6 * BLK, rows), f32),
                pltpu.VMEM((6 * BLK, HD), half),
                pltpu.SemaphoreType.DMA((8,)),
            ],
        ),
        compiler_params=pltpu.CompilerParams(
            dimension_semantics=("arbitrary",), vmem_limit_bytes=56 * 1024 * 1024
        ),
        name="attend_backward",
    )(vertical, columns, offsets, pos, q, g, bk, bv, pk, pv, k, v, far)


def scatter_kernel(
    ydim, zdim, heads, vert, dq, gbk, gbv, gpk, gpv, gok, gov, gfar,
    out_q, out_k, out_v,
    r1, s2, r2, ra, ru, rd, su, sd, tz, zs, zrv, sa, sb, s_up, s_dn, s_mid, s_zs, s_zr, fin,
    local_sem, q_s, q_r, r1_s, r1_r, r2_s, r2_r, d2_s, d2_r, d1_s, d1_r, z_s, z_r, sink_s, sink_r,
    o_s, o_r,
):
    s, y, z, nxt, prv, zl, zr, yu, yd = peers_of(ydim, zdim)
    h = lax.axis_index("head")
    total = ydim * zdim
    local = gok.shape[0]
    step = local // CHUNKS
    f32, half = jnp.float32, jnp.bfloat16
    hz = zdim // 2
    share = dq.shape[0] // heads
    qw = dq.shape[1]
    peers = [(s, lax.rem(h + d, heads)) for d in range(1, heads)]
    meet([(nxt, h), (prv, h), (zl, h), (zr, h), (yu, h), (yd, h)] + peers)

    flying = []
    rot = h // 2

    def chunk(c):
        return pl.ds(lax.rem(rot + c, CHUNKS) * step, step)

    def row(r):
        return lax.rem(r + ydim, ydim) * zdim

    up2 = pl.ds(row(y + 2), hz)
    dn2 = pl.ds(row(y + 2) + hz, hz)
    flying.append(send(gfar.at[up2], ra.at[pl.ds(0, hz)], d2_s.at[0], d2_r.at[0], yu, h))
    flying.append(send(gfar.at[dn2], ra.at[pl.ds(hz, hz)], d2_s.at[1], d2_r.at[1], yd, h))

    @pl.when(y == 2)
    def _():
        send(gfar.at[total], sa, sink_s.at[0], sink_r.at[0], yu, h)

    for c in range(CHUNKS):
        part = chunk(c)
        flying.append(send(gbk.at[part], r1.at[0, c], r1_s.at[0, c], r1_r.at[0, c], prv, h))
        flying.append(send(gbv.at[part], r1.at[1, c], r1_s.at[1, c], r1_r.at[1, c], prv, h))

    flying.append(
        send(gfar.at[pl.ds(row(y + 1) + hz, hz)], ru.at[pl.ds(hz, hz)], d1_s.at[0], d1_r.at[0], yu, h)
    )
    flying.append(
        send(gfar.at[pl.ds(row(y - 1), hz)], rd.at[pl.ds(0, hz)], d1_s.at[1], d1_r.at[1], yd, h)
    )

    @pl.when(y == 1)
    def _():
        send(gfar.at[total], sb, sink_s.at[1], sink_r.at[1], yd, h)

    cols = pl.ds(pl.multiple_of(h * qw, qw), qw)
    for d in range(1, heads):
        peer = lax.rem(h + d, heads)
        rows = pl.ds(pl.multiple_of(peer * share, share), share)
        flying.append(send(dq.at[rows], out_q.at[:, cols], q_s.at[d - 1], q_r.at[d - 1], s, peer))
    mine = pltpu.make_async_copy(
        dq.at[pl.ds(pl.multiple_of(h * share, share), share)], out_q.at[:, cols], local_sem.at[0]
    )
    mine.start()

    landed(ra.at[pl.ds(0, hz)], d2_s.at[0], d2_r.at[0], yd, h)
    su[...] = (
        gfar[pl.ds(row(y + 1), hz)].astype(f32) + ra[pl.ds(0, hz)].astype(f32)
    ).astype(half)
    flying.append(send(su, ru.at[pl.ds(0, hz)], d1_s.at[2], d1_r.at[2], yu, h))

    @pl.when(y == 3)
    def _():
        landed(sa, sink_s.at[0], sink_r.at[0], yd, h)
        s_up[...] = (gfar[total].astype(f32) + sa[...].astype(f32)).astype(half)
        send(s_up, s_dn, sink_s.at[2], sink_r.at[2], yu, h)

    landed(ra.at[pl.ds(hz, hz)], d2_s.at[1], d2_r.at[1], yu, h)
    sd[...] = (
        gfar[pl.ds(row(y - 1) + hz, hz)].astype(f32) + ra[pl.ds(hz, hz)].astype(f32)
    ).astype(half)
    flying.append(send(sd, rd.at[pl.ds(hz, hz)], d1_s.at[3], d1_r.at[3], yd, h))

    for c in range(CHUNKS):
        part = chunk(c)
        landed(r1.at[0, c], r1_s.at[0, c], r1_r.at[0, c], nxt, h)
        s2[0, c] = (gpk[part] + r1[0, c].astype(f32)).astype(half)
        flying.append(send(s2.at[0, c], r2.at[0, c], r2_s.at[0, c], r2_r.at[0, c], prv, h))
        landed(r1.at[1, c], r1_s.at[1, c], r1_r.at[1, c], nxt, h)
        s2[1, c] = (gpv[part] + r1[1, c].astype(f32)).astype(half)
        flying.append(send(s2.at[1, c], r2.at[1, c], r2_s.at[1, c], r2_r.at[1, c], prv, h))

    landed(ru.at[pl.ds(hz, hz)], d1_s.at[0], d1_r.at[0], yd, h)
    landed(ru.at[pl.ds(0, hz)], d1_s.at[2], d1_r.at[2], yd, h)
    landed(rd.at[pl.ds(0, hz)], d1_s.at[1], d1_r.at[1], yu, h)
    landed(rd.at[pl.ds(hz, hz)], d1_s.at[3], d1_r.at[3], yu, h)
    tz[...] = gfar[pl.ds(row(y), zdim)].astype(f32) + ru[...].astype(f32) + rd[...].astype(f32)

    @pl.when(y == 0)
    def _():
        landed(sb, sink_s.at[1], sink_r.at[1], yu, h)
        landed(s_dn, sink_s.at[2], sink_r.at[2], yd, h)
        s_mid[...] = gfar[total].astype(f32) + sb[...].astype(f32) + s_dn[...].astype(f32)

    for t in range(zdim):
        place = lax.rem(z + 2 * zdim - 1 - t, zdim)
        carries = (y == 0) & (place == 0)
        if t > 0:
            landed(zrv.at[t - 1], z_s.at[t - 1], z_r.at[t - 1], zl, h)
        if t < zdim - 1:
            value = tz[place]
            if t > 0:
                value = value + zrv[t - 1].astype(f32)
            zs[t] = value.astype(half)
            flying.append(send(zs.at[t], zrv.at[t], z_s.at[t], z_r.at[t], zr, h))

            @pl.when(carries)
            def _():
                if t > 0:
                    landed(s_zr, sink_s.at[3], sink_r.at[3], zl, h)
                    s_zs[...] = (s_mid[...] + s_zr[...].astype(f32)).astype(half)
                else:
                    s_zs[...] = s_mid[...].astype(half)
                send(s_zs, s_zr, sink_s.at[3], sink_r.at[3], zr, h)

    got = tz[z] + zrv[zdim - 2].astype(f32)
    tz[z] = got
    first = s == 0

    @pl.when(first)
    def _():
        landed(s_zr, sink_s.at[3], sink_r.at[3], zl, h)
        s_mid[...] = s_mid[...] + s_zr[...].astype(f32)

    @pl.when(s != 0)
    def _():
        s_mid[...] = jnp.zeros_like(s_mid)

    own_vert = vert[s]
    width = HD
    ocols = pl.ds(pl.multiple_of(h * width, width), width)
    core = lax.rem(h, 2)
    other = rot * 2 + 1 - core
    same_at = pl.multiple_of(core * share, share)
    other_at = pl.multiple_of((1 - core) * share, share)
    for c in range(CHUNKS):
        at = lax.rem(rot + c, CHUNKS)
        for n, (grad, out) in enumerate(((gok, out_k), (gov, out_v))):
            landed(r2.at[n, c], r2_s.at[n, c], r2_r.at[n, c], nxt, h)
            for i in range(step):
                block = at * step + i
                value = grad[block] + r2[n, c, i].astype(f32)
                value = value + jnp.where(own_vert == block, tz[z, n], 0.0)
                value = value + jnp.where(block == 0, s_mid[n], 0.0)
                fin[n, c, pl.ds(i * BLK, BLK), :] = value.astype(half)
            if c == 0:
                send(fin.at[n, 0, pl.ds(other_at, share)], out.at[:, ocols], o_s.at[n, 0], o_r.at[n, 0], s, other)
                pltpu.make_async_copy(
                    fin.at[n, 0, pl.ds(same_at, share)], out.at[:, ocols], local_sem.at[1 + n]
                ).start()
            else:
                for dest_core in range(2):
                    flying.append(
                        send(
                            fin.at[n, c, pl.ds(dest_core * share, share)],
                            out.at[:, ocols],
                            o_s.at[n, 2 * c + dest_core],
                            o_r.at[n, 2 * c + core],
                            s,
                            at * 2 + dest_core,
                        )
                    )

    for d in range(1, heads):
        source = lax.rem(h + heads - d, heads)
        landed(
            out_q.at[:, pl.ds(pl.multiple_of(source * qw, qw), qw)],
            q_s.at[d - 1], q_r.at[d - 1], s, source,
        )
    for n, out in enumerate((out_k, out_v)):
        landed(
            out.at[:, pl.ds(pl.multiple_of(other * width, width), width)],
            o_s.at[n, 0], o_r.at[n, 0], s, other,
        )
        for c in range(1, CHUNKS):
            for source_core in range(2):
                source = lax.rem(rot + CHUNKS - c, CHUNKS) * 2 + source_core
                landed(
                    out.at[:, pl.ds(pl.multiple_of(source * width, width), width)],
                    o_s.at[n, 2 * c], o_r.at[n, 2 * c + source_core], s, source,
                )
        pltpu.make_async_copy(
            fin.at[n, 0, pl.ds(same_at, share)], out.at[:, ocols], local_sem.at[1 + n]
        ).wait()
        sent(fin.at[n, 0, pl.ds(other_at, share)], out.at[:, ocols], o_s.at[n, 0], o_r.at[n, 0], s, other)
    mine.wait()

    @pl.when(y == 2)
    def _():
        sent(gfar.at[total], sa, sink_s.at[0], sink_r.at[0], yu, h)

    @pl.when(y == 1)
    def _():
        sent(gfar.at[total], sb, sink_s.at[1], sink_r.at[1], yd, h)

    @pl.when(y == 3)
    def _():
        sent(s_up, s_dn, sink_s.at[2], sink_r.at[2], yu, h)

    @pl.when((y == 0) & (z > 0))
    def _():
        sent(s_zs, s_zr, sink_s.at[3], sink_r.at[3], zr, h)

    for copy in flying:
        copy.wait_send()


def scatter(ydim, zdim, heads, vertical, dq, gbk, gbv, gpk, gpv, gok, gov, gfar):
    tokens, qw = dq.shape
    local, blk, width = gok.shape
    share = tokens // heads
    step = local // CHUNKS
    half, f32 = jnp.bfloat16, jnp.float32
    dma = pltpu.SemaphoreType.DMA
    vmem = pltpu.VMEM
    hz = zdim // 2
    one = (2, blk, width)
    parts = (2, CHUNKS, step, blk, width)
    return pl.pallas_call(
        functools.partial(scatter_kernel, ydim, zdim, heads),
        out_shape=(
            jax.ShapeDtypeStruct((share, heads * qw), half),
            jax.ShapeDtypeStruct((share, heads * width), half),
            jax.ShapeDtypeStruct((share, heads * width), half),
        ),
        in_specs=[pl.BlockSpec(memory_space=pltpu.SMEM)]
        + [pl.BlockSpec(memory_space=ANY)] * 3
        + [pl.BlockSpec(memory_space=vmem)] * 5,
        out_specs=[pl.BlockSpec(memory_space=ANY)] * 3,
        scratch_shapes=[
            vmem(parts, half), vmem(parts, half), vmem(parts, half),
            vmem((zdim,) + one, half), vmem((zdim,) + one, half), vmem((zdim,) + one, half),
            vmem((hz,) + one, half), vmem((hz,) + one, half),
            vmem((zdim,) + one, f32), vmem((zdim - 1,) + one, half), vmem((zdim - 1,) + one, half),
            vmem(one, half), vmem(one, half), vmem(one, half), vmem(one, half),
            vmem(one, f32), vmem(one, half), vmem(one, half),
            vmem((2, CHUNKS, step * blk, width), half),
            dma((3,)), dma((heads - 1,)), dma((heads - 1,)),
            dma((2, CHUNKS)), dma((2, CHUNKS)), dma((2, CHUNKS)), dma((2, CHUNKS)),
            dma((2,)), dma((2,)), dma((4,)), dma((4,)),
            dma((zdim,)), dma((zdim,)), dma((4,)), dma((4,)),
            dma((2, 2 * CHUNKS)), dma((2, 2 * CHUNKS)),
        ],
        compiler_params=pltpu.CompilerParams(collective_id=1, has_side_effects=True),
        name="return_terms",
    )(vertical, dq, gbk, gbv, gpk, gpv, gok, gov, gfar)


def shards(ydim, zdim, heads, queries, keys, values, grad_out, vertical, columns, offsets):
    local = queries.shape[0] // BLK
    s = lax.axis_index("seq")
    k = keys.reshape(local, BLK, HD)
    v = values.reshape(local, BLK, HD)
    own = lax.dynamic_index_in_dim(vertical, s, keepdims=False)
    item = jnp.stack(
        [
            lax.dynamic_index_in_dim(k, own, keepdims=False),
            lax.dynamic_index_in_dim(v, own, keepdims=False),
        ]
    )
    pk, pv, bk, bv, far = gather(ydim, zdim, k, v, item)
    pos = s.astype(jnp.int32).reshape(1)
    terms = attend(
        vertical, columns.reshape(-1), offsets.reshape(-1), pos,
        queries, grad_out, bk, bv, pk, pv, k, v, far,
    )
    return scatter(ydim, zdim, heads, vertical, *terms)


def solution(mesh):
    seq, heads = mesh.shape["seq"], mesh.shape["head"]
    spread = P("seq", "head")
    out = P(("seq", "head"), None)
    return jax.shard_map(
        functools.partial(shards, seq // ZDIM, ZDIM, heads),
        mesh=mesh,
        in_specs=(spread, spread, spread, spread, P(), P("seq", None), P("seq", None)),
        out_specs=(out, out, out),
        check_vma=False,
    )
```

```python
import functools
import math

import jax
import jax.numpy as jnp
from jax import lax
from jax.experimental import pallas as pl
from jax.experimental.pallas import tpu as pltpu
from jax.sharding import PartitionSpec as P

HD = 128
BLK = 128
ZDIM = 8
CHUNKS = 4
NEG = -1e30
BIG = 1e30
MESH = pl.DeviceIdType.MESH
ANY = pl.ANY


def peers_of(ydim, zdim):
    s = lax.axis_index("seq")
    total = ydim * zdim
    y, z = s // zdim, lax.rem(s, zdim)
    nxt = lax.rem(s + 1, total)
    prv = lax.rem(s + total - 1, total)
    zl = y * zdim + lax.rem(z + zdim - 1, zdim)
    zr = y * zdim + lax.rem(z + 1, zdim)
    yu = lax.rem(y + 1, ydim) * zdim + z
    yd = lax.rem(y + ydim - 1, ydim) * zdim + z
    return s, y, z, nxt, prv, zl, zr, yu, yd


def send(src, dst, send_sem, recv_sem, seq, head):
    copy = pltpu.make_async_remote_copy(
        src_ref=src,
        dst_ref=dst,
        send_sem=send_sem,
        recv_sem=recv_sem,
        device_id={"seq": seq, "head": head},
        device_id_type=MESH,
    )
    copy.start()
    return copy


def landed(ref, send_sem, recv_sem, seq, head):
    pltpu.make_async_remote_copy(
        src_ref=ref,
        dst_ref=ref,
        send_sem=send_sem,
        recv_sem=recv_sem,
        device_id={"seq": seq, "head": head},
        device_id_type=MESH,
    ).wait_recv()


def sent(src, dst, send_sem, recv_sem, seq, head):
    pltpu.make_async_remote_copy(
        src_ref=src,
        dst_ref=dst,
        send_sem=send_sem,
        recv_sem=recv_sem,
        device_id={"seq": seq, "head": head},
        device_id_type=MESH,
    ).wait_send()


def meet(pairs):
    barrier = pltpu.get_barrier_semaphore()
    for seq, head in pairs:
        pl.semaphore_signal(
            barrier, inc=1, device_id={"seq": seq, "head": head}, device_id_type=MESH
        )
    pl.semaphore_wait(barrier, len(pairs))


def gather_kernel(
    ydim, zdim, k, v, item, pk, pv, bk, bv, far,
    local_sem, own_s, own_r, rel_s, rel_r, z_s, z_r, y_s, y_r, sink_s, sink_r,
):
    s, y, z, nxt, prv, zl, zr, yu, yd = peers_of(ydim, zdim)
    h = lax.axis_index("head")
    total = ydim * zdim
    step = k.shape[0] // CHUNKS
    sink = far.at[total]
    meet([(nxt, h), (prv, h), (zl, h), (zr, h), (yu, h), (yd, h)])

    own = []
    for c in range(CHUNKS):
        part = pl.ds(c * step, step)
        own.append(send(k.at[part], pk.at[part], own_s.at[0, c], own_r.at[0, c], nxt, h))
        own.append(send(v.at[part], pv.at[part], own_s.at[1, c], own_r.at[1, c], nxt, h))
    keep = pltpu.make_async_copy(item, far.at[s], local_sem.at[0])
    keep.start()
    sink_k = pltpu.make_async_copy(k.at[0], far.at[total, 0], local_sem.at[1])
    sink_v = pltpu.make_async_copy(v.at[0], far.at[total, 1], local_sem.at[2])

    @pl.when(s == 0)
    def _():
        sink_k.start()
        sink_v.start()
        sink_k.wait()
        sink_v.wait()

    def item_at(row, t):
        return lax.rem(row + ydim, ydim) * zdim + lax.rem(z + t, zdim)

    def sink_send(origin, slot, seq):
        @pl.when(origin == 0)
        def _():
            send(sink, sink, sink_s.at[slot], sink_r, seq, h)

    def sink_wait(origin):
        @pl.when(origin == 0)
        def _():
            landed(sink, sink_s.at[0], sink_r, prv, h)

    def sink_sent(origin, slot):
        @pl.when(origin == 0)
        def _():
            sent(sink, sink, sink_s.at[slot], sink_r, prv, h)

    flying = []
    events = [(c, n) for c in range(CHUNKS) for n in range(2)]
    near = ((pk, bk), (pv, bv))

    def hop(u, t):
        origin = item_at(y + 1 + u, t)
        landed(far.at[origin], y_s.at[u, t], y_r.at[u, t], yu, h)
        sink_wait(origin)
        if u < ydim - 2:
            flying.append(
                send(far.at[origin], far.at[origin], y_s.at[u + 1, t], y_r.at[u + 1, t], yd, h)
            )
            sink_send(origin, 2 + u, yd)

    for t in range(max(zdim, len(events)) + ydim):
        if t < zdim:
            origin = item_at(y, t)
            src = item if t == 0 else far.at[origin]
            if t > 0:
                landed(far.at[origin], z_s.at[t - 1], z_r.at[t - 1], zr, h)
                sink_wait(origin)
            if t < zdim - 1:
                flying.append(send(src, far.at[origin], z_s.at[t], z_r.at[t], zl, h))
                sink_send(origin, 0, zl)
            flying.append(send(src, far.at[origin], y_s.at[0, t], y_r.at[0, t], yd, h))
            sink_send(origin, 1, yd)
        if t < len(events):
            c, n = events[t]
            part = pl.ds(c * step, step)
            prev, back = near[n]
            landed(prev.at[part], own_s.at[n, c], own_r.at[n, c], prv, h)
            flying.append(send(prev.at[part], back.at[part], rel_s.at[n, c], rel_r.at[n, c], nxt, h))
        for u in range(ydim - 1):
            if 0 <= t - 1 - u < zdim:
                hop(u, t - 1 - u)

    for c, n in events:
        part = pl.ds(c * step, step)
        landed(near[n][1].at[part], rel_s.at[n, c], rel_r.at[n, c], prv, h)
    for copy in own + flying:
        copy.wait_send()
    for t in range(zdim):
        origin = item_at(y, t)
        if t < zdim - 1:
            sink_sent(origin, 0)
        sink_sent(origin, 1)
        for u in range(ydim - 2):
            sink_sent(item_at(y + 1 + u, t), 2 + u)
    keep.wait()


def gather(ydim, zdim, k, v, item):
    blocks = jax.ShapeDtypeStruct(k.shape, k.dtype)
    total = ydim * zdim
    dma = pltpu.SemaphoreType.DMA
    return pl.pallas_call(
        functools.partial(gather_kernel, ydim, zdim),
        out_shape=(
            blocks, blocks, blocks, blocks,
            jax.ShapeDtypeStruct((total + 1,) + item.shape, item.dtype),
        ),
        in_specs=[pl.BlockSpec(memory_space=ANY)] * 2 + [pl.BlockSpec(memory_space=pltpu.VMEM)],
        out_specs=[pl.BlockSpec(memory_space=ANY)] * 5,
        scratch_shapes=[
            dma((3,)),
            dma((2, CHUNKS)), dma((2, CHUNKS)), dma((2, CHUNKS)), dma((2, CHUNKS)),
            dma((zdim,)), dma((zdim,)),
            dma((ydim - 1, zdim)), dma((ydim - 1, zdim)),
            dma((ydim,)), dma,
        ],
        compiler_params=pltpu.CompilerParams(collective_id=0, has_side_effects=True),
        name="gather_blocks",
    )(k, v, item)


def attend_kernel(
    vert, cols, offs, pos,
    q_ref, g_ref, bk, bv, pk, pv, ok, ov, far,
    dq_ref, gbk, gbv, gpk, gpv, gok, gov, gfar,
    kpool, vpool, acck, accv, s_buf, p_buf, e_buf, d_buf, h_buf, sems,
):
    b = pl.program_id(0)
    nb = pl.num_programs(0)
    local = ok.shape[0]
    nfar = far.shape[0]
    group = q_ref.shape[1] // HD
    near = 3 * local
    rows = group * BLK

    @pl.when(b == 0)
    def _():
        copies = []
        for n, (ksrc, vsrc) in enumerate(((bk, bv), (pk, pv), (ok, ov))):
            part = pl.ds(n * local, local)
            copies.append(pltpu.make_async_copy(ksrc, kpool.at[part], sems.at[2 * n]))
            copies.append(pltpu.make_async_copy(vsrc, vpool.at[part], sems.at[2 * n + 1]))
        part = pl.ds(near, nfar)
        copies.append(pltpu.make_async_copy(far.at[:, 0], kpool.at[part], sems.at[6]))
        copies.append(pltpu.make_async_copy(far.at[:, 1], vpool.at[part], sems.at[7]))
        for copy in copies:
            copy.start()
        acck[...] = jnp.zeros_like(acck)
        accv[...] = jnp.zeros_like(accv)
        for copy in copies:
            copy.wait()

    me = pos[0] * local + b
    o0, o1 = offs[2 * b], offs[2 * b + 1]
    c0, c1 = cols[2 * b], cols[2 * b + 1]
    b2, b3 = me - o0, me - o1
    b4, b5 = c0 * local + vert[c0], c1 * local + vert[c1]
    index = [
        near + nfar - 1,
        2 * local + b,
        2 * local + b - o0,
        2 * local + b - o1,
        near + c0,
        near + c1,
    ]
    live = [
        me > 0,
        None,
        (b2 > 0) & (b2 < me),
        (b3 > 0) & (b3 < me) & (b3 != b2),
        (b4 > 0) & (b4 < me) & (b4 != b2) & (b4 != b3),
        (b5 > 0) & (b5 < me) & (b5 != b2) & (b5 != b3) & (b5 != b4),
    ]
    scale = 1.0 / math.sqrt(HD)
    rate = scale * math.log2(math.e)
    nt = (((1,), (1,)), ((), ()))
    f32 = jnp.float32

    qs = jnp.concatenate([q_ref[:, g * HD : (g + 1) * HD] for g in range(group)], axis=0)
    gs = jnp.concatenate([g_ref[:, g * HD : (g + 1) * HD] for g in range(group)], axis=0)
    key_at = lax.broadcasted_iota(jnp.int32, (BLK, rows), 0)
    row_at = lax.broadcasted_iota(jnp.int32, (BLK, rows), 1) & (BLK - 1)
    causal = key_at <= row_at

    top = jnp.full((1, rows), NEG, f32)
    for j in range(6):
        part = pl.ds(j * BLK, BLK)
        kj = kpool[index[j]]
        h_buf[part, :] = kj
        sj = lax.dot_general(kj, qs, nt, preferred_element_type=f32)
        if j == 1:
            sj = jnp.where(causal, sj, NEG)
        s_buf[part, :] = sj
        best = jnp.max(sj, axis=0, keepdims=True)
        if live[j] is not None:
            best = jnp.where(live[j], best, NEG)
        top = jnp.maximum(top, best)
        d_buf[part, :] = lax.dot_general(vpool[index[j]], gs, nt, preferred_element_type=f32)
    total = jnp.zeros((1, rows), f32)
    cross = jnp.zeros((1, rows), f32)
    for j in range(6):
        part = pl.ds(j * BLK, BLK)
        base = top if live[j] is None else jnp.where(live[j], top, BIG)
        ej = jnp.exp2((s_buf[part, :] - base) * rate)
        s_buf[part, :] = ej
        total = total + jnp.sum(ej, axis=0, keepdims=True)
        cross = cross + jnp.sum(ej * d_buf[part, :], axis=0, keepdims=True)
    inv = 1.0 / total
    delta = cross * inv
    inv_scaled = inv * scale
    for j in range(6):
        part = pl.ds(j * BLK, BLK)
        ej = s_buf[part, :]
        p_buf[part, :] = (ej * inv).astype(jnp.bfloat16)
        e_buf[part, :] = ((ej * inv_scaled) * (d_buf[part, :] - delta)).astype(jnp.bfloat16)
    for j in range(6):
        part = pl.ds(j * BLK, BLK)
        acck[index[j]] += jnp.dot(e_buf[part, :], qs, preferred_element_type=f32)
        accv[index[j]] += jnp.dot(p_buf[part, :], gs, preferred_element_type=f32)
    dq = lax.dot_general(
        h_buf[...], e_buf[...], (((0,), (0,)), ((), ())), preferred_element_type=f32
    )
    for g in range(group):
        dq_ref[:, g * HD : (g + 1) * HD] = (
            dq[:, g * BLK : (g + 1) * BLK].T.astype(jnp.bfloat16)
        )

    @pl.when(b == nb - 1)
    def _():
        half = jnp.bfloat16
        gbk[...] = acck[0:local].astype(half)
        gbv[...] = accv[0:local].astype(half)
        gpk[...] = acck[local : 2 * local]
        gpv[...] = accv[local : 2 * local]
        gok[...] = acck[2 * local : near]
        gov[...] = accv[2 * local : near]
        gfar[:, 0] = acck[near : near + nfar].astype(half)
        gfar[:, 1] = accv[near : near + nfar].astype(half)


def attend(vertical, columns, offsets, pos, q, g, bk, bv, pk, pv, k, v, far):
    local = k.shape[0]
    nfar = far.shape[0]
    pool = 3 * local + nfar
    width = q.shape[1]
    rows = width // HD * BLK
    row_spec = pl.BlockSpec((BLK, width), lambda b, *_: (b, 0))
    hbm = pl.BlockSpec(memory_space=ANY)
    f32, half = jnp.float32, jnp.bfloat16

    def whole(shape):
        return pl.BlockSpec(shape, lambda b, *_: (0,) * len(shape), pipeline_mode=pl.Buffered(1))

    near_shape = (local, BLK, HD)
    far_shape = (nfar, 2, BLK, HD)
    return pl.pallas_call(
        attend_kernel,
        out_shape=(
            jax.ShapeDtypeStruct(q.shape, half),
            jax.ShapeDtypeStruct(near_shape, half),
            jax.ShapeDtypeStruct(near_shape, half),
            jax.ShapeDtypeStruct(near_shape, f32),
            jax.ShapeDtypeStruct(near_shape, f32),
            jax.ShapeDtypeStruct(near_shape, f32),
            jax.ShapeDtypeStruct(near_shape, f32),
            jax.ShapeDtypeStruct(far_shape, half),
        ),
        grid_spec=pltpu.PrefetchScalarGridSpec(
            num_scalar_prefetch=4,
            grid=(local,),
            in_specs=[row_spec, row_spec] + [hbm] * 7,
            out_specs=[row_spec] + [whole(near_shape)] * 6 + [whole(far_shape)],
            scratch_shapes=[
                pltpu.VMEM((pool, BLK, HD), half),
                pltpu.VMEM((pool, BLK, HD), half),
                pltpu.VMEM((pool, BLK, HD), f32),
                pltpu.VMEM((pool, BLK, HD), f32),
                pltpu.VMEM((6 * BLK, rows), f32),
                pltpu.VMEM((6 * BLK, rows), half),
                pltpu.VMEM((6 * BLK, rows), half),
                pltpu.VMEM((6 * BLK, rows), f32),
                pltpu.VMEM((6 * BLK, HD), half),
                pltpu.SemaphoreType.DMA((8,)),
            ],
        ),
        compiler_params=pltpu.CompilerParams(
            dimension_semantics=("arbitrary",), vmem_limit_bytes=56 * 1024 * 1024
        ),
        name="attend_backward",
    )(vertical, columns, offsets, pos, q, g, bk, bv, pk, pv, k, v, far)


def scatter_kernel(
    ydim, zdim, heads, vert, dq, gbk, gbv, gpk, gpv, gok, gov, gfar,
    out_q, out_k, out_v,
    r1, s2, r2, prev_in, own_in, y_in, y_out, tz, z_in, z_out,
    sink_in, sink_out, sink_ring, sink_pass, sink_sum, fin,
    local_sem, q_s, q_r, r1_s, r1_r, r2_s, r2_r, y_s, y_r, z_s, z_r, sink_s, sink_r,
    o_s, o_r,
):
    s, y, z, nxt, prv, zl, zr, yu, yd = peers_of(ydim, zdim)
    h = lax.axis_index("head")
    total = ydim * zdim
    local = gok.shape[0]
    step = local // CHUNKS
    f32, half = jnp.float32, jnp.bfloat16
    share = dq.shape[0] // heads
    qw = dq.shape[1]
    peers = [(s, lax.rem(h + d, heads)) for d in range(1, heads)]
    meet([(nxt, h), (prv, h), (zl, h), (zr, h), (yu, h), (yd, h)] + peers)

    flying = []
    rot = h // 2
    events = [(c, n) for c in range(CHUNKS) for n in range(2)]

    def chunk(c):
        return pl.ds(lax.rem(rot + c, CHUNKS) * step, step)

    for c, n in events:
        src = (gbk, gbv)[n]
        flying.append(send(src.at[chunk(c)], r1.at[n, c], r1_s.at[n, c], r1_r.at[n, c], prv, h))
    loads = [
        pltpu.make_async_copy(src, dst, local_sem.at[3 + i])
        for i, (src, dst) in enumerate(
            ((gpk, prev_in.at[0]), (gpv, prev_in.at[1]), (gok, own_in.at[0]), (gov, own_in.at[1]))
        )
    ]
    for copy in loads:
        copy.start()

    def place_of(t):
        return lax.rem(z + 2 * zdim - 1 - t, zdim)

    def term(r, t):
        return gfar.at[lax.rem(y + ydim - r, ydim) * zdim + place_of(t)]

    def y_first(t):
        flying.append(send(term(1, t), y_in.at[0, t], y_s.at[0, t], y_r.at[0, t], yu, h))

        @pl.when((y == 1) & (place_of(t) == 0))
        def _():
            send(gfar.at[total], sink_in, sink_s.at[0], sink_r.at[0], yu, h)

    def y_hop(u, t):
        landed(y_in.at[u - 1, t], y_s.at[u - 1, t], y_r.at[u - 1, t], yd, h)
        value = term(u + 1, t)[...].astype(f32) + y_in[u - 1, t].astype(f32)
        if u < ydim - 1:
            y_out[u - 1, t] = value.astype(half)
            flying.append(
                send(y_out.at[u - 1, t], y_in.at[u, t], y_s.at[u, t], y_r.at[u, t], yu, h)
            )
            sink_here = (y == u + 1) & (place_of(t) == 0)
        else:
            tz[t] = value
            sink_here = (y == 0) & (place_of(t) == 0)

        @pl.when(sink_here)
        def _():
            landed(sink_in, sink_s.at[0], sink_r.at[0], yd, h)
            sum_ = gfar[total].astype(f32) + sink_in[...].astype(f32)
            if u < ydim - 1:
                sink_out[...] = sum_.astype(half)
                send(sink_out, sink_in, sink_s.at[0], sink_r.at[0], yu, h)
            else:
                sink_sum[...] = sum_

    def z_hop(t):
        if t > 0:
            landed(z_in.at[t - 1], z_s.at[t - 1], z_r.at[t - 1], zl, h)
            tz[t] = tz[t] + z_in[t - 1].astype(f32)
        if t < zdim - 1:
            z_out[t] = tz[t].astype(half)
            flying.append(send(z_out.at[t], z_in.at[t], z_s.at[t], z_r.at[t], zr, h))

            @pl.when((y == 0) & (place_of(t) == 0))
            def _():
                if t > 0:
                    landed(sink_ring, sink_s.at[1], sink_r.at[1], zl, h)
                    sink_pass[...] = (sink_sum[...] + sink_ring[...].astype(f32)).astype(half)
                else:
                    sink_pass[...] = sink_sum[...].astype(half)
                send(sink_pass, sink_ring, sink_s.at[1], sink_r.at[1], zr, h)

    y_first(0)
    y_first(1)

    cols = pl.ds(pl.multiple_of(h * qw, qw), qw)
    for d in range(1, heads):
        peer = lax.rem(h + d, heads)
        rows = pl.ds(pl.multiple_of(peer * share, share), share)
        flying.append(send(dq.at[rows], out_q.at[:, cols], q_s.at[d - 1], q_r.at[d - 1], s, peer))
    mine = pltpu.make_async_copy(
        dq.at[pl.ds(pl.multiple_of(h * share, share), share)], out_q.at[:, cols], local_sem.at[0]
    )
    mine.start()

    for i in range(max(zdim, len(events)) + ydim + 1):
        if i + 2 < zdim:
            y_first(i + 2)
        for u in range(1, ydim):
            if 0 <= i + 1 - u < zdim:
                y_hop(u, i + 1 - u)
        if 0 <= i - ydim + 1 < zdim:
            z_hop(i - ydim + 1)
        if i < len(events):
            c, n = events[i]
            if c == 0:
                loads[n].wait()
            landed(r1.at[n, c], r1_s.at[n, c], r1_r.at[n, c], nxt, h)
            s2[n, c] = (prev_in[n, chunk(c)] + r1[n, c].astype(f32)).astype(half)
            flying.append(send(s2.at[n, c], r2.at[n, c], r2_s.at[n, c], r2_r.at[n, c], prv, h))

    @pl.when(s == 0)
    def _():
        landed(sink_ring, sink_s.at[1], sink_r.at[1], zl, h)
        sink_sum[...] = sink_sum[...] + sink_ring[...].astype(f32)

    @pl.when(s != 0)
    def _():
        sink_sum[...] = jnp.zeros_like(sink_sum)

    loads[2].wait()
    loads[3].wait()
    own_vert = vert[s]
    width = HD
    ocols = pl.ds(pl.multiple_of(h * width, width), width)
    core = lax.rem(h, 2)
    other = rot * 2 + 1 - core
    same_at = pl.multiple_of(core * share, share)
    other_at = pl.multiple_of((1 - core) * share, share)
    for c in range(CHUNKS):
        at = lax.rem(rot + c, CHUNKS)
        for n, out in enumerate((out_k, out_v)):
            landed(r2.at[n, c], r2_s.at[n, c], r2_r.at[n, c], nxt, h)
            for i in range(step):
                block = at * step + i
                value = own_in[n, block] + r2[n, c, i].astype(f32)
                value = value + jnp.where(own_vert == block, tz[zdim - 1, n], 0.0)
                value = value + jnp.where(block == 0, sink_sum[n], 0.0)
                fin[n, c, pl.ds(i * BLK, BLK), :] = value.astype(half)
            if c == 0:
                send(fin.at[n, 0, pl.ds(other_at, share)], out.at[:, ocols], o_s.at[n, 0], o_r.at[n, 0], s, other)
                pltpu.make_async_copy(
                    fin.at[n, 0, pl.ds(same_at, share)], out.at[:, ocols], local_sem.at[1 + n]
                ).start()
            else:
                for dest_core in range(2):
                    flying.append(
                        send(
                            fin.at[n, c, pl.ds(dest_core * share, share)],
                            out.at[:, ocols],
                            o_s.at[n, 2 * c + dest_core],
                            o_r.at[n, 2 * c + core],
                            s,
                            at * 2 + dest_core,
                        )
                    )

    for d in range(1, heads):
        source = lax.rem(h + heads - d, heads)
        landed(
            out_q.at[:, pl.ds(pl.multiple_of(source * qw, qw), qw)],
            q_s.at[d - 1], q_r.at[d - 1], s, source,
        )
    for n, out in enumerate((out_k, out_v)):
        landed(
            out.at[:, pl.ds(pl.multiple_of(other * width, width), width)],
            o_s.at[n, 0], o_r.at[n, 0], s, other,
        )
        for c in range(1, CHUNKS):
            for source_core in range(2):
                source = lax.rem(rot + CHUNKS - c, CHUNKS) * 2 + source_core
                landed(
                    out.at[:, pl.ds(pl.multiple_of(source * width, width), width)],
                    o_s.at[n, 2 * c], o_r.at[n, 2 * c + source_core], s, source,
                )
        pltpu.make_async_copy(
            fin.at[n, 0, pl.ds(same_at, share)], out.at[:, ocols], local_sem.at[1 + n]
        ).wait()
        sent(fin.at[n, 0, pl.ds(other_at, share)], out.at[:, ocols], o_s.at[n, 0], o_r.at[n, 0], s, other)
    mine.wait()

    @pl.when(y > 0)
    def _():
        sent(sink_out, sink_in, sink_s.at[0], sink_r.at[0], yu, h)

    @pl.when((y == 0) & (z > 0))
    def _():
        sent(sink_pass, sink_ring, sink_s.at[1], sink_r.at[1], zr, h)

    for copy in flying:
        copy.wait_send()


def scatter(ydim, zdim, heads, vertical, dq, gbk, gbv, gpk, gpv, gok, gov, gfar):
    tokens, qw = dq.shape
    local, blk, width = gok.shape
    share = tokens // heads
    step = local // CHUNKS
    half, f32 = jnp.bfloat16, jnp.float32
    dma = pltpu.SemaphoreType.DMA
    vmem = pltpu.VMEM
    hz = zdim // 2
    one = (2, blk, width)
    parts = (2, CHUNKS, step, blk, width)
    return pl.pallas_call(
        functools.partial(scatter_kernel, ydim, zdim, heads),
        out_shape=(
            jax.ShapeDtypeStruct((share, heads * qw), half),
            jax.ShapeDtypeStruct((share, heads * width), half),
            jax.ShapeDtypeStruct((share, heads * width), half),
        ),
        in_specs=[pl.BlockSpec(memory_space=pltpu.SMEM)]
        + [pl.BlockSpec(memory_space=ANY)] * 7
        + [pl.BlockSpec(memory_space=vmem)],
        out_specs=[pl.BlockSpec(memory_space=ANY)] * 3,
        scratch_shapes=[
            vmem(parts, half), vmem(parts, half), vmem(parts, half),
            vmem((2, local, blk, width), f32), vmem((2, local, blk, width), f32),
            vmem((ydim - 1, zdim) + one, half), vmem((ydim - 2, zdim) + one, half),
            vmem((zdim,) + one, f32), vmem((zdim - 1,) + one, half), vmem((zdim - 1,) + one, half),
            vmem(one, half), vmem(one, half), vmem(one, half), vmem(one, half), vmem(one, f32),
            vmem((2, CHUNKS, step * blk, width), half),
            dma((7,)), dma((heads - 1,)), dma((heads - 1,)),
            dma((2, CHUNKS)), dma((2, CHUNKS)), dma((2, CHUNKS)), dma((2, CHUNKS)),
            dma((ydim - 1, zdim)), dma((ydim - 1, zdim)),
            dma((zdim,)), dma((zdim,)), dma((2,)), dma((2,)),
            dma((2, 2 * CHUNKS)), dma((2, 2 * CHUNKS)),
        ],
        compiler_params=pltpu.CompilerParams(collective_id=1, has_side_effects=True),
        name="return_terms",
    )(vertical, dq, gbk, gbv, gpk, gpv, gok, gov, gfar)


def shards(ydim, zdim, heads, queries, keys, values, grad_out, vertical, columns, offsets):
    local = queries.shape[0] // BLK
    s = lax.axis_index("seq")
    k = keys.reshape(local, BLK, HD)
    v = values.reshape(local, BLK, HD)
    own = lax.dynamic_index_in_dim(vertical, s, keepdims=False)
    item = jnp.stack(
        [
            lax.dynamic_index_in_dim(k, own, keepdims=False),
            lax.dynamic_index_in_dim(v, own, keepdims=False),
        ]
    )
    pk, pv, bk, bv, far = gather(ydim, zdim, k, v, item)
    pos = s.astype(jnp.int32).reshape(1)
    terms = attend(
        vertical, columns.reshape(-1), offsets.reshape(-1), pos,
        queries, grad_out, bk, bv, pk, pv, k, v, far,
    )
    return scatter(ydim, zdim, heads, vertical, *terms)


def solution(mesh):
    seq, heads = mesh.shape["seq"], mesh.shape["head"]
    spread = P("seq", "head")
    out = P(("seq", "head"), None)
    return jax.shard_map(
        functools.partial(shards, seq // ZDIM, ZDIM, heads),
        mesh=mesh,
        in_specs=(spread, spread, spread, spread, P(), P("seq", None), P("seq", None)),
        out_specs=(out, out, out),
        check_vma=False,
    )
```
